32 devices in a mesh: groups: 2 (over x), tensor: 8 (over z, y), dp: 2 (over core).
Axes of the slice: x: 2, y: 2, z: 4, core: 2. Of those that a mesh axis runs over, the one named last changes fastest.
Arguments:
- activations: bfloat16 [512, 8192], P(('groups', 'dp'), 'tensor'), parts along dimension 0, may hold values from -640 to 640
- norm_gain: bfloat16 [8192], replicated, may hold values from 0.25 to 1.75
- gate_frozen_weight: bfloat16 [14336, 8192], P(('tensor', 'dp')), may hold values from -0.0625 to 0.0625
- up_frozen_weight: bfloat16 [14336, 8192], P(('tensor', 'dp')), may hold values from -0.0625 to 0.0625
- down_weight: bfloat16 [14336, 8192], P(('tensor', 'dp')), may hold values from -0.046875 to 0.046875
- cotangent: bfloat16 [512, 8192], P(('groups', 'dp'), 'tensor'), parts along dimension 0, may hold values from -6 to 6
- squeeze_master: float32 [256, 8192], P('groups', ('tensor', 'dp')), parts along dimension 0, may hold values from -0.0625 to 0.0625
- squeeze_first: float32 [256, 8192], P('groups', ('tensor', 'dp')), parts along dimension 0, may hold values from -100 to 100
- squeeze_second: float32 [256, 8192], P('groups', ('tensor', 'dp')), parts along dimension 0, may hold values from 100 to 2000
- expand_master: float32 [28672, 128], P(('groups', 'tensor', 'dp')), parts along dimension 0, may hold values from -0.75 to 0.75
- expand_first: float32 [28672, 128], P(('groups', 'tensor', 'dp')), parts along dimension 0, may hold values from -9 to 9
- expand_second: float32 [28672, 128], P(('groups', 'tensor', 'dp')), parts along dimension 0, may hold values from 0.5 to 10
Outputs:
- input_grad: float32 [512, 8192], P(('groups', 'dp'), 'tensor'), parts along dimension 0
- squeeze_master_new: float32 [256, 8192], P('groups', ('tensor', 'dp')), parts along dimension 0
- squeeze_first_new: float32 [256, 8192], P('groups', ('tensor', 'dp')), parts along dimension 0
- squeeze_second_new: float32 [256, 8192], P('groups', ('tensor', 'dp')), parts along dimension 0
- squeeze_adapter: bfloat16 [256, 8192], P('groups', 'tensor'), parts along dimension 0
- expand_master_new: float32 [28672, 128], P(('groups', 'tensor', 'dp')), parts along dimension 0
- expand_first_new: float32 [28672, 128], P(('groups', 'tensor', 'dp')), parts along dimension 0
- expand_second_new: float32 [28672, 128], P(('groups', 'tensor', 'dp')), parts along dimension 0
- expand_adapter: bfloat16 [28672, 128], P(('groups', 'tensor', 'dp')), parts along dimension 0
The draws below stay inside these ranges and needn't reach their ends.
There are 2 independent parts, one for each index of `groups`. The reference program is written for one: setup_inputs(seed, part) draws one part's arguments, and reference() takes and returns one part's arrays. A program takes and returns all parts, laid end to end along the dimension named above; an argument that names none is the same for every part. Nothing has to cross between parts.
All inputs are finite; a program needn't handle non-finite values.
Results may differ from the reference program's by a relative error of at most 0.0055.
Values may be sent and summed in bfloat16 or wider, within the bound.
No kernel may reach another device: no remote copies, remote signals or barrier semaphores. Data moves between devices by JAX's collectives and lax.ppermute only.
A program may use at most 128 MiB of HBM per device.

```python
import math
import jax
import jax.numpy as jnp
from jax import lax

D = 8192
FFW = 14336
R = 64
STEP = 20
TOKENS = 256


def draw_activations(key, part):
    first_key, second_key = jax.random.split(jax.random.fold_in(key, 7))
    columns = 10.0 ** (jnp.arange(D, dtype=jnp.float32) / D)
    values = jnp.clip(jax.random.normal(first_key, (TOKENS, D), jnp.float32), -4.0, 4.0)
    row_scales = 10.0 ** jax.random.uniform(second_key, (TOKENS, 1), jnp.float32)
    return (values * row_scales * columns[None, :]).astype(jnp.bfloat16)


def steps_of(key, dims, pieces, low, largest):
    level = 1.0
    for axis_at, blocks in pieces:
        heights = jax.random.uniform(jax.random.fold_in(jax.random.fold_in(key, 6), axis_at), (blocks,), jnp.float32, low / len(pieces), largest / len(pieces))
        level = level * jnp.repeat(jnp.exp(heights), dims[axis_at] // blocks).reshape((-1,) + (1,) * (len(dims) - 1 - axis_at))
    return level


def scatter_about(own_key, extent, spread, limit, cuts=(), kind=jnp.bfloat16):
    array = spread * jax.random.normal(own_key, extent, jnp.float32)
    if cuts:
        array = array * steps_of(own_key, extent, cuts, -0.22, 0.18)
    return jnp.clip(array, -limit, limit).astype(kind)


def setup_inputs(seed: int = 0, part: int = 0) -> dict:
    splits = jax.random.split(jax.random.key(seed), 13)
    part_keys = jax.random.split(jax.random.fold_in(splits[12], part), 13)
    return {
        "activations": draw_activations(jax.random.fold_in(jax.random.fold_in(splits[12], part), 71), part),
        "norm_gain": jnp.clip(1.0 + 0.15 * jax.random.normal(splits[1], (D,), jnp.float32), 0.25, 1.75).astype(jnp.bfloat16),
        "gate_frozen_weight": scatter_about(splits[2], (FFW, D), D ** -0.5, 0.0625, ((0, 16),)),
        "up_frozen_weight": scatter_about(splits[3], (FFW, D), D ** -0.5, 0.0625, ((0, 16),)),
        "down_weight": scatter_about(splits[4], (FFW, D), FFW ** -0.5, 0.046875, ((0, 16),)),
        "cotangent": scatter_about(part_keys[5], (TOKENS, D), 1.0, 6.0, ((0, 2), (1, 8))),
        "squeeze_master": scatter_about(part_keys[6], (2 * R, D), D ** -0.5, 0.0625, ((1, 16),), jnp.float32),
        "squeeze_first": scatter_about(part_keys[7], (2 * R, D), 20.0, 100.0, ((1, 16),), jnp.float32),
        "squeeze_second": jnp.clip(jnp.exp(math.log(2000.0) - 2.9957323 * jax.random.uniform(part_keys[8], (2 * R, D), jnp.float32) ** steps_of(part_keys[8], (2 * R, D), ((1, 16),), -0.2, 0.2)), 100.0, 2000.0),
        "expand_master": scatter_about(part_keys[9], (FFW, 2 * R), R ** -0.5, 0.75, ((0, 16),), jnp.float32),
        "expand_first": scatter_about(part_keys[10], (FFW, 2 * R), 1.5, 9.0, ((0, 16),), jnp.float32),
        "expand_second": jnp.clip(jnp.exp(math.log(10.0) - 2.9957323 * jax.random.uniform(part_keys[11], (FFW, 2 * R), jnp.float32) ** steps_of(part_keys[11], (FFW, 2 * R), ((0, 16),), -0.2, 0.2)), 0.5, 10.0),
    }


adapter_output_scale = 0.25
norm_epsilon = 1e-05
learning_rate = 0.001
decay_rate = 0.1
beta_first = 0.9
beta_second = 0.95
adam_epsilon = 1e-08

def adamw_update(master, first, second, grads):
    first_new = beta_first * first + (1.0 - beta_first) * grads
    second_new = beta_second * second + (1.0 - beta_second) * grads * grads
    first_hat = first_new / (1.0 - beta_first ** STEP)
    second_hat = second_new / (1.0 - beta_second ** STEP)
    master_new = master - learning_rate * (first_hat / (jnp.sqrt(second_hat) + adam_epsilon) + decay_rate * master)
    return (master_new, first_new, second_new)

def reference(activations, norm_gain, gate_frozen_weight, up_frozen_weight, down_weight, cotangent, squeeze_master, squeeze_first, squeeze_second, expand_master, expand_first, expand_second):
    input_float = activations.astype(jnp.float32)
    gain_float = norm_gain.astype(jnp.float32)
    scale_rows = lax.rsqrt(lax.optimization_barrier(jnp.mean(input_float * input_float, axis=1)) + norm_epsilon)
    normalized_rows = (input_float * scale_rows[:, None] * gain_float).astype(jnp.bfloat16)
    squeeze_current = squeeze_master.astype(jnp.bfloat16)
    expand_factor_now = expand_master.astype(jnp.bfloat16)
    adapter_inner_rank = expand_factor_now.shape[1] // 2
    reduced_features = jnp.dot(normalized_rows, squeeze_current.T, preferred_element_type=jnp.float32).astype(jnp.bfloat16)
    gate_preactivation = jnp.dot(normalized_rows, gate_frozen_weight.T, preferred_element_type=jnp.float32) + adapter_output_scale * jnp.dot(reduced_features[:, :adapter_inner_rank], expand_factor_now[:, :adapter_inner_rank].T, preferred_element_type=jnp.float32)
    up_preactivation = jnp.dot(normalized_rows, up_frozen_weight.T, preferred_element_type=jnp.float32) + adapter_output_scale * jnp.dot(reduced_features[:, adapter_inner_rank:], expand_factor_now[:, adapter_inner_rank:].T, preferred_element_type=jnp.float32)
    hidden_grad = jnp.dot(cotangent, down_weight.T, preferred_element_type=jnp.float32)
    sigmoid_gate = jax.nn.sigmoid(gate_preactivation)
    gate_branch_gradient = (hidden_grad * up_preactivation * sigmoid_gate * (1.0 + gate_preactivation * (1.0 - sigmoid_gate))).astype(jnp.bfloat16)
    up_branch_gradient = (hidden_grad * gate_preactivation * sigmoid_gate).astype(jnp.bfloat16)
    reduced_gradient = adapter_output_scale * jnp.concatenate([jnp.dot(gate_branch_gradient, expand_factor_now[:, :adapter_inner_rank], preferred_element_type=jnp.float32), jnp.dot(up_branch_gradient, expand_factor_now[:, adapter_inner_rank:], preferred_element_type=jnp.float32)], axis=1)
    reduced_gradient = reduced_gradient.astype(jnp.bfloat16)
    normed_grad = jnp.dot(gate_branch_gradient, gate_frozen_weight, preferred_element_type=jnp.float32) + jnp.dot(up_branch_gradient, up_frozen_weight, preferred_element_type=jnp.float32) + jnp.dot(reduced_gradient, squeeze_current, preferred_element_type=jnp.float32)
    row_dot = lax.optimization_barrier(jnp.sum(normed_grad * input_float * gain_float, axis=1))
    input_grad = scale_rows[:, None] * gain_float * normed_grad - input_float * (scale_rows ** 3)[:, None] * row_dot[:, None] / D
    squeeze_grad = jnp.dot(reduced_gradient.T, normalized_rows, preferred_element_type=jnp.float32)
    expand_factor_gradient = adapter_output_scale * jnp.concatenate([jnp.dot(gate_branch_gradient.T, reduced_features[:, :adapter_inner_rank], preferred_element_type=jnp.float32), jnp.dot(up_branch_gradient.T, reduced_features[:, adapter_inner_rank:], preferred_element_type=jnp.float32)], axis=1)
    squeeze_new, squeeze_first_new, squeeze_second_new = adamw_update(squeeze_master, squeeze_first, squeeze_second, squeeze_grad)
    expand_new, expand_first_new, expand_second_new = adamw_update(expand_master, expand_first, expand_second, expand_factor_gradient)
    return (input_grad, squeeze_new, squeeze_first_new, squeeze_second_new, squeeze_new.astype(jnp.bfloat16), expand_new, expand_first_new, expand_second_new, expand_new.astype(jnp.bfloat16))
```

```python
import functools

import jax
import jax.numpy as jnp
from jax import lax
from jax.experimental import pallas as pl
from jax.experimental.pallas import tpu as pltpu
from jax.sharding import PartitionSpec as P

STEP = 20


adapter_output_scale = 0.25
norm_epsilon = 1e-05
learning_rate = 0.001
decay_rate = 0.1
beta_first = 0.9
beta_second = 0.95
adam_epsilon = 1e-08

MIB = 1024 * 1024
NT = (((1,), (1,)), ((), ()))
TN = (((0,), (0,)), ((), ()))
f32 = jnp.float32
bf16 = jnp.bfloat16


def dot_nt(a, b):
    return lax.dot_general(a, b, NT, preferred_element_type=f32)


def dot_tn(a, b):
    return lax.dot_general(a, b, TN, preferred_element_type=f32)


def dot_nn(a, b):
    return jnp.dot(a, b, preferred_element_type=f32)


def adamw_update(master, first, second, grads):
    first_new = beta_first * first + (1.0 - beta_first) * grads
    second_new = beta_second * second + (1.0 - beta_second) * grads * grads
    first_hat = first_new / (1.0 - beta_first**STEP)
    second_hat = second_new / (1.0 - beta_second**STEP)
    master_new = master - learning_rate * (
        first_hat / (jnp.sqrt(second_hat) + adam_epsilon) + decay_rate * master
    )
    return (master_new, first_new, second_new)


def halves(x):
    lane = lax.broadcasted_iota(jnp.int32, x.shape, 1)
    zero = jnp.zeros_like(x)
    gate = lane < x.shape[1] // 2
    return jnp.where(gate, x, zero), jnp.where(gate, zero, x)


def normalize(rows, scale, gain):
    return (rows.astype(f32) * scale * gain.astype(f32)).astype(bf16)


VMEM = pl.BlockSpec(memory_space=pltpu.VMEM)
ANY = pl.BlockSpec(memory_space=pl.ANY)
SMEM = pl.BlockSpec(memory_space=pltpu.SMEM)


def params(mib):
    return pltpu.CompilerParams(vmem_limit_bytes=mib * MIB)


def column_copies(ids_ref, arrays, slots, sems, count, width):
    copies = []
    for i in range(count):
        start = pl.multiple_of(ids_ref[i] * width, 128)
        for j, array in enumerate(arrays):
            copies.append(
                pltpu.make_async_copy(
                    array.at[:, pl.ds(start, width)], slots.at[i, j], sems.at[i, j]
                )
            )
    for copy in copies:
        copy.start()
    return copies


def forward_call(ids, slabs, scales, gain, weights, sums, last):
    count = len(slabs)
    rows, width = slabs[0][0].shape
    hidden = weights[0].shape[0]
    n_in = 4 * count

    def kernel(*refs):
        ids_ref = refs[0]
        slab_refs = [refs[1 + 4 * i : 5 + 4 * i] for i in range(count)]
        at = 1 + n_in
        scale_own, scale_far, gain_ref = refs[at : at + 3]
        weight_refs = refs[at + 3 : at + 6]
        at += 6
        sum_refs = refs[at : at + 3] if sums is not None else None
        at += 3 if sums is not None else 0
        if last is not None:
            low_own, low_far, expand = refs[at : at + 3]
            at += 3
        outs = refs[at : at + (4 if last is not None else 3)]
        slots, sems = refs[-2:]
        copies = column_copies(ids_ref, weight_refs, slots, sems, count, width)
        totals = [r[...] for r in sum_refs] if sum_refs is not None else [None] * 3
        for i, (act, cot, act_far, cot_far) in enumerate(slab_refs):
            start = pl.multiple_of(ids_ref[i] * width, 128)
            gain_row = gain_ref[:, pl.ds(start, width)]
            normed = jnp.concatenate(
                [
                    normalize(act[...], scale_own[...], gain_row),
                    normalize(act_far[...], scale_far[...], gain_row),
                ],
                axis=0,
            )
            rows_cot = jnp.concatenate([cot[...], cot_far[...]], axis=0)
            for j, left in enumerate((normed, normed, rows_cot)):
                copies[3 * i + j].wait()
                part = dot_nt(left, slots[i, j])
                totals[j] = part if totals[j] is None else totals[j] + part
        if last is None:
            for out, total in zip(outs, totals):
                out[...] = total
            return
        gate_out, up_out, hidden_grad = totals
        low = jnp.concatenate([low_own[...], low_far[...]], axis=0)
        low_gate, low_up = halves(low)
        factor_gate, factor_up = halves(expand[...].astype(bf16))
        gate = gate_out + adapter_output_scale * dot_nt(low_gate, factor_gate)
        up = up_out + adapter_output_scale * dot_nt(low_up, factor_up)
        sig = jax.nn.sigmoid(gate)
        hs = hidden_grad * sig
        gate_grad = (hidden_grad * up * sig * (1.0 + gate * (1.0 - sig))).astype(bf16)
        up_grad = (hs * gate).astype(bf16)
        low_grad = adapter_output_scale * (
            dot_nn(gate_grad, factor_gate) + dot_nn(up_grad, factor_up)
        )
        dots = jnp.sum(
            gate_grad.astype(f32) * gate_out + up_grad.astype(f32) * up_out,
            axis=1,
            keepdims=True,
        )
        dots = jnp.transpose(jnp.broadcast_to(dots, (2 * rows, 128)))
        gate_ref, up_ref, own_ref, far_ref = outs
        gate_ref[...] = gate_grad
        up_ref[...] = up_grad
        own_ref[:rows, :] = low_grad[:rows]
        own_ref[rows:, :] = dots[:8, :rows]
        far_ref[:rows, :] = low_grad[rows:]
        far_ref[rows:, :] = dots[:8, rows:]

    args = [ids]
    for slab in slabs:
        args += list(slab)
    args += [scales[0], scales[1], gain, *weights]
    specs = [SMEM] + [VMEM] * (n_in + 3) + [ANY] * 3
    aliases = {}
    if sums is not None:
        if last is None:
            aliases = {len(args) + j: j for j in range(3)}
        args += list(sums)
        specs += [VMEM] * 3
    if last is not None:
        args += list(last)
        specs += [VMEM] * 3
        rank = last[2].shape[1]
        out_shape = [jax.ShapeDtypeStruct((2 * rows, hidden), bf16)] * 2
        out_shape += [jax.ShapeDtypeStruct((rows + 8, rank), f32)] * 2
    else:
        out_shape = [jax.ShapeDtypeStruct((2 * rows, hidden), f32)] * 3
    return pl.pallas_call(
        kernel,
        out_shape=out_shape,
        in_specs=specs,
        out_specs=[VMEM] * len(out_shape),
        scratch_shapes=[
            pltpu.VMEM((count, 3, hidden, width), bf16),
            pltpu.SemaphoreType.DMA((count, 3)),
        ],
        input_output_aliases=aliases,
        compiler_params=params(44),
        cost_estimate=pl.CostEstimate(
            flops=count * 12 * rows * width * hidden,
            transcendentals=0,
            bytes_accessed=count * 6 * width * hidden,
        ),
        name="forward_last" if last is not None else "forward_part",
    )(*args)


def backward_call(ids, grads, weights, count, width):
    hidden = weights[0].shape[0]
    rows = grads[0].shape[0] // 2

    def kernel(ids_ref, gate_ref, up_ref, w_gate, w_up, *refs):
        outs = refs[: 2 * count]
        slots, sems = refs[-2:]
        copies = column_copies(ids_ref, (w_gate, w_up), slots, sems, count, width)
        for i in range(count):
            copies[2 * i].wait()
            part = dot_nn(gate_ref[...], slots[i, 0])
            copies[2 * i + 1].wait()
            part = part + dot_nn(up_ref[...], slots[i, 1])
            outs[2 * i][...] = part[:rows]
            outs[2 * i + 1][...] = part[rows:].astype(bf16)

    return pl.pallas_call(
        kernel,
        out_shape=[
            jax.ShapeDtypeStruct((rows, width), f32),
            jax.ShapeDtypeStruct((rows, width), bf16),
        ]
        * count,
        in_specs=[SMEM, VMEM, VMEM, ANY, ANY],
        out_specs=[VMEM] * (2 * count),
        scratch_shapes=[
            pltpu.VMEM((count, 2, hidden, width), bf16),
            pltpu.SemaphoreType.DMA((count, 2)),
        ],
        compiler_params=params(28),
        cost_estimate=pl.CostEstimate(
            flops=count * 8 * rows * width * hidden,
            transcendentals=0,
            bytes_accessed=count * 4 * width * hidden,
        ),
        name="backward_part",
    )(ids, *grads, *weights)


def low_rank_call(act, scale, gain, index, squeeze):
    rows, width = act.shape

    def kernel(index_ref, act_ref, scale_ref, gain_ref, squeeze_ref, out):
        start = pl.multiple_of(index_ref[0] * width, 128)
        normed = normalize(act_ref[...], scale_ref[...], gain_ref[:, pl.ds(start, width)])
        out[...] = dot_nt(normed, squeeze_ref[...])

    return pl.pallas_call(
        kernel,
        out_shape=jax.ShapeDtypeStruct((rows, squeeze.shape[0]), f32),
        in_specs=[SMEM, VMEM, VMEM, VMEM, VMEM],
        out_specs=VMEM,
        compiler_params=params(8),
        name="low_rank",
    )(index, act, scale, gain, squeeze)


def first_sends(own, far):
    rows, width = own.shape
    half = width // 2

    def kernel(own_ref, far_ref, a, b):
        total = (own_ref[...] + far_ref[...].astype(f32)).astype(bf16)
        a[...] = total[:, :half]
        b[...] = total[:, half:]

    return pl.pallas_call(
        kernel,
        out_shape=[jax.ShapeDtypeStruct((rows, half), bf16)] * 2,
        in_specs=[VMEM] * 2,
        out_specs=[VMEM] * 2,
        compiler_params=params(8),
        name="first_sends",
    )(own, far)


def next_sends(right, left, got):
    rows, width = right[0].shape
    part = got[0].shape[1]

    def kernel(ro, rf, lo, lf, gr, gl, a, b):
        if part == width:
            a[...] = (ro[...] + rf[...].astype(f32) + gr[...].astype(f32)).astype(bf16)
            b[...] = (lo[...] + lf[...].astype(f32) + gl[...].astype(f32)).astype(bf16)
            return
        right_sum = ro[...] + rf[...].astype(f32)
        left_sum = lo[...] + lf[...].astype(f32)
        a[:, :part] = (right_sum[:, :part] + gr[...].astype(f32)).astype(bf16)
        a[:, part:] = right_sum[:, part:].astype(bf16)
        b[:, :part] = left_sum[:, :part].astype(bf16)
        b[:, part:] = (left_sum[:, part:] + gl[...].astype(f32)).astype(bf16)

    return pl.pallas_call(
        kernel,
        out_shape=[jax.ShapeDtypeStruct((rows, width), bf16)] * 2,
        in_specs=[VMEM] * 6,
        out_specs=[VMEM] * 2,
        compiler_params=params(12),
        name="next_sends",
    )(*right, *left, *got)


def input_grad_call(index, own, far, got, act, scale, gain, low, low_rank, dots, squeeze):
    rows, width = act.shape
    model_width = gain.shape[1]

    def kernel(idx, own_ref, far_ref, gr, gl, act_ref, scale_ref, gain_ref, low_ref, rank_ref, dots_ref, sq_ref, out):
        start = pl.multiple_of(idx[0] * width, 128)
        gain_row = gain_ref[:, pl.ds(start, width)].astype(f32)
        grad = own_ref[...] + far_ref[...].astype(f32) + gr[...].astype(f32) + gl[...].astype(f32)
        grad = grad + dot_nn(low_ref[...], sq_ref[...])
        scale_col = scale_ref[...]
        total = dots_ref[...] + jnp.sum(low_ref[...].astype(f32) * rank_ref[...], axis=1, keepdims=True)
        factor = scale_col * scale_col * total / model_width
        out[...] = scale_col * gain_row * grad - act_ref[...].astype(f32) * factor

    return pl.pallas_call(
        kernel,
        out_shape=jax.ShapeDtypeStruct((rows, width), f32),
        in_specs=[SMEM] + [VMEM] * 11,
        out_specs=VMEM,
        compiler_params=params(16),
        name="input_grad",
    )(index, own, far, *got, act, scale, gain, low, low_rank, dots, squeeze)


def expand_call(grads, low_own, low_far, master, first, second):
    hidden, rank = master.shape
    rows2 = grads[0].shape[0]
    blocks = hidden // 128 if hidden % 128 == 0 else 1
    tile = hidden // blocks

    def kernel(gate_ref, up_ref, lo, lf, p_ref, m_ref, v_ref, p_out, m_out, v_out, b_out):
        low = jnp.concatenate([lo[...], lf[...]], axis=0)
        low_gate, low_up = halves(low)
        grad = adapter_output_scale * (
            dot_tn(gate_ref[...], low_gate) + dot_tn(up_ref[...], low_up)
        )
        p, m, v = adamw_update(p_ref[...], m_ref[...], v_ref[...], grad)
        p_out[...] = p
        m_out[...] = m
        v_out[...] = v
        b_out[...] = p.astype(bf16)

    wide = pl.BlockSpec((rows2, tile), lambda i: (0, i))
    whole = pl.BlockSpec(low_own.shape, lambda i: (0, 0))
    tall = pl.BlockSpec((tile, rank), lambda i: (i, 0))
    return pl.pallas_call(
        kernel,
        grid=(blocks,),
        out_shape=[jax.ShapeDtypeStruct((hidden, rank), f32)] * 3
        + [jax.ShapeDtypeStruct((hidden, rank), bf16)],
        in_specs=[wide, wide, whole, whole, tall, tall, tall],
        out_specs=[tall] * 4,
        compiler_params=params(16),
        name="expand_adam",
    )(*grads, low_own, low_far, master, first, second)


def squeeze_call(indices, low_own, low_far, act_own, act_far, scales, gain, master, first, second):
    rank, cols = master.shape
    rows = act_own.shape[0]

    def kernel(idx, lo, lf, ao, af, so, sf, gain_ref, p_ref, m_ref, v_ref, p_out, m_out, v_out, b_out):
        start = pl.multiple_of(idx[0] * cols, 128)
        gain_row = gain_ref[:, pl.ds(pl.multiple_of(idx[1] * cols, 128), cols)]
        own = normalize(ao[:, pl.ds(start, cols)], so[...], gain_row)
        far = normalize(af[:, pl.ds(start, cols)], sf[...], gain_row)
        grad = dot_tn(lo[...], own) + dot_tn(lf[...], far)
        p, m, v = adamw_update(p_ref[...], m_ref[...], v_ref[...], grad)
        p_out[...] = p
        m_out[...] = m
        v_out[...] = v
        b_out[...] = p.astype(bf16)

    return pl.pallas_call(
        kernel,
        out_shape=[jax.ShapeDtypeStruct((rank, cols), f32)] * 3
        + [jax.ShapeDtypeStruct((rank, cols), bf16)],
        in_specs=[SMEM] + [VMEM] * 10,
        out_specs=[VMEM] * 4,
        compiler_params=params(16),
        name="squeeze_adam",
    )(indices, low_own, low_far, act_own, act_far, *scales, gain, master, first, second)


def ring_of(size):
    if size % 2 == 0 and size <= 8:
        return [2 * q for q in range(size // 2)] + [2 * q + 1 for q in range(size // 2)][::-1]
    return list(range(size))


def on_device(
    size,
    activations,
    norm_gain,
    gate_frozen_weight,
    up_frozen_weight,
    down_weight,
    cotangent,
    squeeze_master,
    squeeze_first,
    squeeze_second,
    expand_master,
    expand_first,
    expand_second,
):
    model_width = norm_gain.shape[0]
    rows, width = activations.shape
    half = size // 2
    order = ring_of(size)
    place = [order.index(i) for i in range(size)]
    right = [(order[i], order[(i + 1) % size]) for i in range(size)]
    left = [(b, a) for a, b in right]
    tensor_index = lax.axis_index("tensor")
    data_index = lax.axis_index("dp")
    here = jnp.asarray(place, jnp.int32)[tensor_index]

    def slab_ids(offsets):
        spots = lax.rem(here + size + jnp.asarray(offsets, jnp.int32), size)
        return jnp.asarray(order, jnp.int32)[spots]

    def to_right(x):
        return lax.ppermute(x, "tensor", right)

    def to_left(x):
        return lax.ppermute(x, "tensor", left)

    def across(x):
        return lax.ppermute(x, "dp", [(0, 1), (1, 0)])

    def sum_over_tensor(x):
        step = 1
        while step < size:
            x = x + lax.ppermute(x, "tensor", [(i, i ^ step) for i in range(size)])
            step *= 2
        return x

    gain = norm_gain.reshape(1, model_width)
    weights = (gate_frozen_weight, up_frozen_weight, down_weight)
    own_index = tensor_index.reshape(1).astype(jnp.int32)

    act_r = act_l = activations
    cot_r = cot_l = cotangent
    got = []
    for step in range(1, half + 1):
        if step < half:
            act_r, cot_r, act_l, cot_l = lax.optimization_barrier(
                (to_right(act_r), to_right(cot_r), to_left(act_l), to_left(cot_l))
            )
            got.append((act_r, cot_r, act_l, cot_l))
        else:
            act_r, cot_l = lax.optimization_barrier((to_right(act_r), to_left(cot_l)))
            got.append((act_r, cot_l))

    act_float = activations.astype(f32)
    squares = sum_over_tensor(jnp.sum(act_float * act_float, axis=1).reshape(1, rows))
    scale_row = lax.rsqrt(squares / model_width + norm_epsilon)
    scale_own = scale_row.reshape(rows, 1)
    scale_far = across(scale_row).reshape(rows, 1)
    scales = (scale_own, scale_far)

    squeeze_half = squeeze_master.astype(bf16)
    squeeze_other = across(squeeze_half)
    first_core = data_index == 0
    squeeze_slab = jnp.concatenate(
        [
            jnp.where(first_core, squeeze_half, squeeze_other),
            jnp.where(first_core, squeeze_other, squeeze_half),
        ],
        axis=1,
    )
    low_rank = sum_over_tensor(
        low_rank_call(activations, scale_own, gain, own_index, squeeze_slab)
    )
    low_own = low_rank.astype(bf16)
    low_far = across(low_own)

    act_far = across(activations)
    own_slab = (activations, cotangent, act_far, across(cotangent))
    sums = None
    slabs, offsets = [own_slab], [0]
    for step in range(1, half):
        a_r, c_r, a_l, c_l = got[step - 1]
        slabs += [(a_r, c_r, across(a_r), across(c_r)), (a_l, c_l, across(a_l), across(c_l))]
        offsets += [-step, step]
        sums = forward_call(slab_ids(offsets), slabs, scales, gain, weights, sums, None)
        slabs, offsets = [], []
    a_r, c_l = got[half - 1]
    grads = forward_call(
        slab_ids([half]),
        [(a_r, c_l, across(a_r), across(c_l))],
        scales,
        gain,
        weights,
        sums,
        (low_own, low_far, expand_master),
    )
    gate_grad, up_grad, low_part, low_other = grads
    grads = (gate_grad, up_grad)

    low_sum = sum_over_tensor(low_part + across(low_other))
    low_grad_own = low_sum[:rows].astype(bf16)
    low_grad_far = across(low_grad_own)
    dots = low_sum[rows].reshape(rows, 1)

    pair = weights[:2]
    (own, other) = backward_call(slab_ids([half]), grads, pair, 1, width)
    send_r, send_l = first_sends(own, across(other))
    got_r, got_l = lax.optimization_barrier((to_right(send_r), to_left(send_l)))
    for distance in range(half - 1, 0, -1):
        ro, rx, lo, lx = backward_call(slab_ids([distance, -distance]), grads, pair, 2, width)
        send_r, send_l = next_sends((ro, across(rx)), (lo, across(lx)), (got_r, got_l))
        got_r, got_l = lax.optimization_barrier((to_right(send_r), to_left(send_l)))
    own, other = backward_call(own_index, grads, pair, 1, width)

    expand_new, expand_first_new, expand_second_new, expand_adapter = expand_call(
        grads, low_own, low_far, expand_master, expand_first, expand_second
    )
    squeeze_index = jnp.stack([data_index, 2 * tensor_index + data_index]).astype(jnp.int32)
    squeeze_new, squeeze_first_new, squeeze_second_new, adapter_half = squeeze_call(
        squeeze_index,
        low_grad_own,
        low_grad_far,
        activations,
        act_far,
        scales,
        gain,
        squeeze_master,
        squeeze_first,
        squeeze_second,
    )
    adapter_other = across(adapter_half)
    squeeze_adapter = jnp.concatenate(
        [
            jnp.where(first_core, adapter_half, adapter_other),
            jnp.where(first_core, adapter_other, adapter_half),
        ],
        axis=1,
    )
    input_grad = input_grad_call(
        own_index,
        own,
        across(other),
        (got_r, got_l),
        activations,
        scale_own,
        gain,
        low_grad_own,
        low_rank,
        dots,
        squeeze_slab,
    )
    return (
        input_grad,
        squeeze_new,
        squeeze_first_new,
        squeeze_second_new,
        squeeze_adapter,
        expand_new,
        expand_first_new,
        expand_second_new,
        expand_adapter,
    )


def solution(mesh):
    placed = (
        P(("groups", "dp"), "tensor"),
        P(),
        P(("tensor", "dp"), None),
        P(("tensor", "dp"), None),
        P(("tensor", "dp"), None),
        P(("groups", "dp"), "tensor"),
        P("groups", ("tensor", "dp")),
        P("groups", ("tensor", "dp")),
        P("groups", ("tensor", "dp")),
        P(("groups", "tensor", "dp"), None),
        P(("groups", "tensor", "dp"), None),
        P(("groups", "tensor", "dp"), None),
    )
    return jax.shard_map(
        functools.partial(on_device, mesh.shape["tensor"]),
        mesh=mesh,
        in_specs=placed,
        out_specs=(
            P(("groups", "dp"), "tensor"),
            P("groups", ("tensor", "dp")),
            P("groups", ("tensor", "dp")),
            P("groups", ("tensor", "dp")),
            P("groups", "tensor"),
            P(("groups", "tensor", "dp"), None),
            P(("groups", "tensor", "dp"), None),
            P(("groups", "tensor", "dp"), None),
            P(("groups", "tensor", "dp"), None),
        ),
        check_vma=False,
    )
```

```python
import jax
import jax.numpy as jnp
from jax import lax
from jax.experimental import pallas as pl
from jax.experimental.pallas import tpu as pltpu
from jax.sharding import PartitionSpec as P


STEP = 20


adapter_output_scale = 0.25
norm_epsilon = 1e-05
learning_rate = 0.001
decay_rate = 0.1
beta_first = 0.9
beta_second = 0.95
adam_epsilon = 1e-08

MIB = 1024 * 1024
NT = (((1,), (1,)), ((), ()))
TN = (((0,), (0,)), ((), ()))
f32 = jnp.float32
bf16 = jnp.bfloat16


def dot_nt(a, b):
    return lax.dot_general(a, b, NT, preferred_element_type=f32)


def dot_tn(a, b):
    return lax.dot_general(a, b, TN, preferred_element_type=f32)


def dot_nn(a, b):
    return jnp.dot(a, b, preferred_element_type=f32)


def adamw_update(master, first, second, grads):
    first_new = beta_first * first + (1.0 - beta_first) * grads
    second_new = beta_second * second + (1.0 - beta_second) * grads * grads
    first_hat = first_new / (1.0 - beta_first**STEP)
    second_hat = second_new / (1.0 - beta_second**STEP)
    master_new = master - learning_rate * (
        first_hat / (jnp.sqrt(second_hat) + adam_epsilon) + decay_rate * master
    )
    return (master_new, first_new, second_new)


def halves(x):
    lane = lax.broadcasted_iota(jnp.int32, x.shape, 1)
    zero = jnp.zeros_like(x)
    gate = lane < x.shape[1] // 2
    return jnp.where(gate, x, zero), jnp.where(gate, zero, x)


def normalize(rows, scale, gain):
    return (rows.astype(f32) * scale * gain.astype(f32)).astype(bf16)


VMEM = pl.BlockSpec(memory_space=pltpu.VMEM)
ANY = pl.BlockSpec(memory_space=pl.ANY)
HBM = pl.BlockSpec(memory_space=pltpu.HBM)


def params(mib):
    return pltpu.CompilerParams(vmem_limit_bytes=mib * MIB)


def ring_of(size):
    if size % 2 == 0 and size <= 8:
        return [2 * q for q in range(size // 2)] + [2 * q + 1 for q in range(size // 2)][::-1]
    return list(range(size))


def slab_at(size, offset):
    index = lax.axis_index("tensor")
    if offset == 0:
        return index
    if ring_of(size) == list(range(size)):
        return lax.rem(index + size + offset, size)
    half = size // 2
    odd = lax.rem(index, 2)
    step = lax.div(index, 2)
    place = jnp.where(odd == 0, step, size - 1 - step)
    place = lax.rem(place + size + offset, size)
    return jnp.where(place < half, 2 * place, 2 * (size - 1 - place) + 1)


def begin(sems, pairs):
    copies = [pltpu.make_async_copy(a, b, sems.at[i]) for i, (a, b) in enumerate(pairs)]
    for copy in copies:
        copy.start()
    return copies


def wait(copies):
    for copy in copies:
        copy.wait()


def column(row):
    n = row.shape[1]
    return jnp.transpose(jnp.broadcast_to(row, (n, n)))[:, :1]


def columns_of(array, start, width):
    return array.at[:, pl.ds(pl.multiple_of(start, 128), width)]


def forward_call(size, offsets, slabs, scales, gain, weights, sums, last):
    count = len(slabs)
    rows, width = slabs[0][0].shape
    hidden = weights[0].shape[0]
    n_in = 4 * count

    def kernel(*refs):
        slab_refs = refs[:n_in]
        scale_refs = refs[n_in : n_in + 2]
        gain_ref = refs[n_in + 2]
        weight_refs = refs[n_in + 3 : n_in + 6]
        at = n_in + 6
        sum_refs = refs[at : at + 3] if sums is not None else None
        at += 3 if sums is not None else 0
        if last is not None:
            last_refs = refs[at : at + 3]
            at += 3
        outs = refs[at : at + (4 if last is not None else 3)]
        scratch = refs[at + len(outs) :]
        slab_bufs, scale_bufs, gain_buf, down_bufs, sems = scratch[:5]
        pairs = [(scale_refs[0], scale_bufs.at[0]), (scale_refs[1], scale_bufs.at[1])]
        for i in range(count):
            start = slab_at(size, offsets[i]) * width
            pairs.append((columns_of(gain_ref, start, width), gain_buf.at[i]))
            pairs += [(slab_refs[4 * i + j], slab_bufs.at[i, j]) for j in range(4)]
            pairs.append((columns_of(weight_refs[2], start, width), down_bufs.at[i]))
        if last is not None:
            pairs += [(last_refs[0], scratch[5].at[0]), (last_refs[1], scratch[5].at[1])]
            pairs += [(last_refs[2], scratch[6])]
        copies = begin(sems, pairs)
        wait(copies[:2])
        scale_own = column(scale_bufs[0])
        scale_far = column(scale_bufs[1])
        totals = [None] * 3

        def multiply(i, j, lhs):
            if j == 2:
                part = dot_nt(lhs, down_bufs[i])
            else:
                start = pl.multiple_of(slab_at(size, offsets[i]) * width, 128)
                part = dot_nt(lhs, weight_refs[j][:, pl.ds(start, width)])
            if last is not None:
                totals[j] = sum_refs[j][...] + part
            elif i > 0:
                outs[j][...] += part
            elif sum_refs is not None:
                outs[j][...] = sum_refs[j][...] + part
            else:
                outs[j][...] = part

        for i in range(count):
            wait(copies[2 + 6 * i : 7 + 6 * i])
            gain_row = gain_buf[i]
            normed = jnp.concatenate(
                [
                    normalize(slab_bufs[i, 0], scale_own, gain_row),
                    normalize(slab_bufs[i, 2], scale_far, gain_row),
                ],
                axis=0,
            )
            multiply(i, 0, normed)
            multiply(i, 1, normed)
        for i in range(count):
            copies[7 + 6 * i].wait()
            multiply(i, 2, jnp.concatenate([slab_bufs[i, 1], slab_bufs[i, 3]], axis=0))
        if last is None:
            return
        wait(copies[2 + 6 * count :])
        gate_out, up_out, hidden_grad = totals
        low = jnp.concatenate([scratch[5][0], scratch[5][1]], axis=0)
        low_gate, low_up = halves(low)
        factor_gate, factor_up = halves(scratch[6][...].astype(bf16))
        gate = gate_out + adapter_output_scale * dot_nt(low_gate, factor_gate)
        up = up_out + adapter_output_scale * dot_nt(low_up, factor_up)
        sig = jax.nn.sigmoid(gate)
        gate_grad = (hidden_grad * up * sig * (1.0 + gate * (1.0 - sig))).astype(bf16)
        up_grad = (hidden_grad * gate * sig).astype(bf16)
        gate_ref, up_ref, own_ref, far_ref = outs
        gate_ref[...] = gate_grad
        up_ref[...] = up_grad
        low_grad = adapter_output_scale * (
            dot_nn(gate_grad, factor_gate) + dot_nn(up_grad, factor_up)
        )
        dots = jnp.sum(
            gate_grad.astype(f32) * gate_out + up_grad.astype(f32) * up_out,
            axis=1,
            keepdims=True,
        )
        dots = jnp.transpose(jnp.broadcast_to(dots, (2 * rows, 128)))
        own_ref[:rows, :] = low_grad[:rows]
        own_ref[rows:, :] = dots[:8, :rows]
        far_ref[:rows, :] = low_grad[rows:]
        far_ref[rows:, :] = dots[:8, rows:]

    args = []
    for slab in slabs:
        args += list(slab)
    args += [scales[0], scales[1], gain, *weights]
    specs = [HBM] * (len(args) - 3) + [VMEM, VMEM, HBM]
    aliases = {}
    scratch_shapes = [
        pltpu.VMEM((count, 4, rows, width), bf16),
        pltpu.VMEM((2, 1, rows), f32),
        pltpu.VMEM((count, 1, width), f32),
        pltpu.VMEM((count, hidden, width), bf16),
        pltpu.SemaphoreType.DMA((2 + 6 * count + 3,)),
    ]
    if sums is not None:
        if last is None:
            aliases = {len(args) + j: j for j in range(3)}
        args += list(sums)
        specs += [VMEM] * 3
    if last is not None:
        args += list(last)
        specs += [HBM] * 3
        rank = last[2].shape[1]
        scratch_shapes += [pltpu.VMEM((2, rows, rank), bf16), pltpu.VMEM((hidden, rank), f32)]
        out_shape = [jax.ShapeDtypeStruct((2 * rows, hidden), bf16)] * 2
        out_shape += [jax.ShapeDtypeStruct((rows + 8, rank), f32)] * 2
    else:
        out_shape = [jax.ShapeDtypeStruct((2 * rows, hidden), f32)] * 3
    return pl.pallas_call(
        kernel,
        out_shape=out_shape,
        in_specs=specs,
        out_specs=[VMEM] * len(out_shape),
        scratch_shapes=scratch_shapes,
        input_output_aliases=aliases,
        compiler_params=params(9 if last is None else 12),
        cost_estimate=pl.CostEstimate(
            flops=count * 12 * rows * width * hidden,
            transcendentals=0,
            bytes_accessed=count * 6 * width * hidden,
        ),
        name="forward_last" if last is not None else "forward_part",
    )(*args)


def resident(weight):
    def kernel(source, out, sem):
        copy = pltpu.make_async_copy(source, out, sem)
        copy.start()
        copy.wait()

    return pl.pallas_call(
        kernel,
        out_shape=jax.ShapeDtypeStruct(weight.shape, weight.dtype),
        in_specs=[HBM],
        out_specs=VMEM,
        scratch_shapes=[pltpu.SemaphoreType.DMA],
        compiler_params=params(1),
        name="resident",
    )(weight)


def backward_call(size, offsets, grads, weights, width):
    count = len(offsets)
    hidden = weights[0].shape[0]
    rows = grads[0].shape[0] // 2

    def kernel(gate_hbm, up_hbm, w_gate, w_up, *refs):
        outs = refs[: 2 * count]
        grad_bufs, own_bufs, far_bufs, sems, out_sems = refs[2 * count :]
        copies = begin(sems, [(gate_hbm, grad_bufs.at[0]), (up_hbm, grad_bufs.at[1])])
        wait(copies)
        sent = []
        for i in range(count):
            columns = pl.ds(pl.multiple_of(slab_at(size, offsets[i]) * width, 128), width)
            part = dot_nn(grad_bufs[0], w_gate[:, columns]) + dot_nn(grad_bufs[1], w_up[:, columns])
            far_bufs[i] = part[rows:].astype(bf16)
            own_bufs[i] = part[:rows]
            for j, buf in enumerate((own_bufs, far_bufs)):
                copy = pltpu.make_async_copy(buf.at[i], outs[2 * i + j], out_sems.at[2 * i + j])
                copy.start()
                sent.append(copy)
        wait(sent)

    return pl.pallas_call(
        kernel,
        out_shape=[
            jax.ShapeDtypeStruct((rows, width), f32),
            jax.ShapeDtypeStruct((rows, width), bf16),
        ]
        * count,
        in_specs=[ANY, ANY, VMEM, VMEM],
        out_specs=[ANY] * (2 * count),
        scratch_shapes=[
            pltpu.VMEM((2, 2 * rows, hidden), bf16),
            pltpu.VMEM((count, rows, width), f32),
            pltpu.VMEM((count, rows, width), bf16),
            pltpu.SemaphoreType.DMA((2,)),
            pltpu.SemaphoreType.DMA((2 * count,)),
        ],
        compiler_params=params(6),
        cost_estimate=pl.CostEstimate(
            flops=count * 8 * rows * width * hidden,
            transcendentals=0,
            bytes_accessed=count * 4 * width * hidden,
        ),
        name="backward_part",
    )(*grads, *weights)


def loading(shapes, body, out_shape, out_any, mib):
    n = len(shapes)
    n_out = len(out_shape)

    def kernel(*refs):
        bufs = refs[n + n_out : 2 * n + n_out]
        sems = refs[-1]
        copies = begin(sems, list(zip(refs[:n], bufs)))
        if not out_any:
            body(bufs, refs[n : n + n_out], copies)
            return
        results = refs[2 * n + n_out : 2 * n + 2 * n_out]
        body(bufs, results, copies)
        sent = [
            pltpu.make_async_copy(a, b, sems.at[n + i])
            for i, (a, b) in enumerate(zip(results, refs[n : n + n_out]))
        ]
        for copy in sent:
            copy.start()
        wait(sent)

    scratch = [pltpu.VMEM(x.shape, x.dtype) for x in shapes]
    if out_any:
        scratch += [pltpu.VMEM(x.shape, x.dtype) for x in out_shape]
    scratch.append(pltpu.SemaphoreType.DMA((n + n_out,)))
    return pl.pallas_call(
        kernel,
        out_shape=out_shape,
        in_specs=[HBM] * n,
        out_specs=[ANY if out_any else VMEM] * n_out,
        scratch_shapes=scratch,
        compiler_params=params(mib),
    )


def both_cores(own, other):
    rows, cols = own.shape

    def kernel(own_ref, other_ref, out, sems):
        core = lax.axis_index("dp")
        wait(
            begin(
                sems,
                [
                    (own_ref, columns_of(out, core * cols, cols)),
                    (other_ref, columns_of(out, (1 - core) * cols, cols)),
                ],
            )
        )

    return pl.pallas_call(
        kernel,
        out_shape=jax.ShapeDtypeStruct((rows, 2 * cols), own.dtype),
        in_specs=[HBM] * 2,
        out_specs=ANY,
        scratch_shapes=[pltpu.SemaphoreType.DMA((2,))],
        compiler_params=params(1),
        name="both_cores",
    )(own, other)


def low_rank_call(act, scale, gain, squeeze):
    rows, width = act.shape

    def body(bufs, outs, copies):
        wait(copies)
        act_ref, scale_ref, gain_ref, squeeze_ref = bufs
        start = pl.multiple_of(lax.axis_index("tensor") * width, 128)
        normed = normalize(act_ref[...], column(scale_ref[...]), gain_ref[:, pl.ds(start, width)])
        outs[0][...] = dot_nt(normed, squeeze_ref[...])

    args = (act, scale, gain, squeeze)
    out = [jax.ShapeDtypeStruct((rows, squeeze.shape[0]), f32)]
    return loading(args, body, out, False, 3)(*args)[0]


def first_sends(own, far):
    rows, width = own.shape
    half = width // 2

    def body(bufs, outs, copies):
        wait(copies)
        total = (bufs[0][...] + bufs[1][...].astype(f32)).astype(bf16)
        outs[0][...] = total[:, :half]
        outs[1][...] = total[:, half:]

    args = (own, far)
    out = [jax.ShapeDtypeStruct((rows, half), bf16)] * 2
    return loading(args, body, out, False, 3)(*args)


def next_sends(right, left, got):
    rows, width = right[0].shape
    part = got[0].shape[1]

    def body(bufs, outs, copies):
        ro, rf, lo, lf, gr, gl = bufs
        a, b = outs
        wait([copies[0], copies[1], copies[4]])
        right_sum = ro[...] + rf[...].astype(f32)
        if part == width:
            a[...] = (right_sum + gr[...].astype(f32)).astype(bf16)
        else:
            a[:, :part] = (right_sum[:, :part] + gr[...].astype(f32)).astype(bf16)
            a[:, part:] = right_sum[:, part:].astype(bf16)
        wait([copies[2], copies[3], copies[5]])
        left_sum = lo[...] + lf[...].astype(f32)
        if part == width:
            b[...] = (left_sum + gl[...].astype(f32)).astype(bf16)
        else:
            b[:, :part] = left_sum[:, :part].astype(bf16)
            b[:, part:] = (left_sum[:, part:] + gl[...].astype(f32)).astype(bf16)

    args = (*right, *left, *got)
    out = [jax.ShapeDtypeStruct((rows, width), bf16)] * 2
    return loading(args, body, out, False, 5)(*args)


def input_grad_call(own, far, got, act, scale, gain, low, low_rank, low_sum, squeeze):
    rows, width = act.shape
    model_width = gain.shape[1]

    def body(bufs, outs, copies):
        own_ref, far_ref, gr, gl, act_ref, scale_ref, gain_ref, low_ref, rank_ref, sum_ref, sq_ref = bufs
        wait(copies)
        start = pl.multiple_of(lax.axis_index("tensor") * width, 128)
        gain_row = gain_ref[:, pl.ds(start, width)]
        grad = own_ref[...] + far_ref[...].astype(f32) + gr[...].astype(f32) + gl[...].astype(f32)
        grad = grad + dot_nn(low_ref[...], sq_ref[...])
        scale_col = column(scale_ref[...])
        dots = column(sum_ref[rows : rows + 1, :])
        total = dots + jnp.sum(low_ref[...].astype(f32) * rank_ref[...], axis=1, keepdims=True)
        factor = scale_col * scale_col * total / model_width
        outs[0][...] = scale_col * gain_row * grad - act_ref[...].astype(f32) * factor

    args = (own, far, *got, act, scale, gain, low, low_rank, low_sum, squeeze)
    out = [jax.ShapeDtypeStruct((rows, width), f32)]
    return loading(args, body, out, True, 6)(*args)[0]


def store_adam(p, m, v, outs):
    outs[0][...] = p
    outs[1][...] = m
    outs[2][...] = v
    outs[3][...] = p.astype(bf16)


def expand_call(grads, low_own, low_far, master, first, second):
    hidden, rank = master.shape

    def body(bufs, outs, copies):
        gate_ref, up_ref, lo, lf, p_ref, m_ref, v_ref = bufs
        wait(copies)
        low = jnp.concatenate([lo[...], lf[...]], axis=0)
        low_gate, low_up = halves(low)
        grad = adapter_output_scale * (
            dot_tn(gate_ref[...], low_gate) + dot_tn(up_ref[...], low_up)
        )
        store_adam(*adamw_update(p_ref[...], m_ref[...], v_ref[...], grad), outs)

    args = (*grads, low_own, low_far, master, first, second)
    out = [jax.ShapeDtypeStruct((hidden, rank), f32)] * 3
    out += [jax.ShapeDtypeStruct((hidden, rank), bf16)]
    return loading(args, body, out, True, 8)(*args)


def squeeze_call(low_own, low_far, act_own, act_far, scales, gain, master, first, second):
    rank, cols = master.shape

    def body(bufs, outs, copies):
        lo, lf, ao, af, so, sf, gain_ref, p_ref, m_ref, v_ref = bufs
        wait(copies)
        core = lax.axis_index("dp")
        start = pl.multiple_of(core * cols, 128)
        place = (lax.axis_index("tensor") * 2 + core) * cols
        gain_row = gain_ref[:, pl.ds(pl.multiple_of(place, 128), cols)]
        own = normalize(ao[:, pl.ds(start, cols)], column(so[...]), gain_row)
        far = normalize(af[:, pl.ds(start, cols)], column(sf[...]), gain_row)
        grad = dot_tn(lo[...], own) + dot_tn(lf[...], far)
        store_adam(*adamw_update(p_ref[...], m_ref[...], v_ref[...], grad), outs)

    args = (low_own, low_far, act_own, act_far, *scales, gain, master, first, second)
    out = [jax.ShapeDtypeStruct((rank, cols), f32)] * 3
    out += [jax.ShapeDtypeStruct((rank, cols), bf16)]
    return loading(args, body, out, True, 6)(*args)


def on_device(
    size,
    activations,
    norm_gain,
    gate_frozen_weight,
    up_frozen_weight,
    down_weight,
    cotangent,
    squeeze_master,
    squeeze_first,
    squeeze_second,
    expand_master,
    expand_first,
    expand_second,
):
    model_width = norm_gain.shape[0]
    rows, width = activations.shape
    half = size // 2
    order = ring_of(size)
    right = [(order[i], order[(i + 1) % size]) for i in range(size)]
    left = [(b, a) for a, b in right]

    def to_right(x):
        return lax.ppermute(x, "tensor", right)

    def to_left(x):
        return lax.ppermute(x, "tensor", left)

    def across(x):
        return lax.ppermute(x, "dp", [(0, 1), (1, 0)])

    def sum_over_tensor(x):
        step, stage = 1, 0
        while step < size:
            x = x + lax.ppermute(x, "tensor", [(i, i ^ step) for i in range(size)])
            step *= 2
            stage += 1
        return x

    def in_hbm(x):
        return pltpu.with_memory_space_constraint(x, pltpu.HBM)

    down_weight = in_hbm(down_weight)
    act_hbm, cot_hbm = in_hbm(activations), in_hbm(cotangent)
    squeeze_state = [in_hbm(x) for x in (squeeze_master, squeeze_first, squeeze_second)]
    expand_state = [in_hbm(x) for x in (expand_master, expand_first, expand_second)]

    act_r = act_l = activations
    cot_r = cot_l = cotangent
    got = []
    for step in range(1, half + 1):
        if step < half:
            act_r, cot_r, act_l, cot_l = lax.optimization_barrier(
                (to_right(act_r), to_right(cot_r), to_left(act_l), to_left(cot_l))
            )
            got.append((act_r, cot_r, act_l, cot_l))
        else:
            act_r, cot_l = lax.optimization_barrier((to_right(act_r), to_left(cot_l)))
            got.append((act_r, cot_l))

    gain = norm_gain.astype(f32).reshape(1, model_width)
    act_float = activations.astype(f32)
    squares = jnp.sum(act_float * act_float, axis=1).reshape(1, rows)
    squares = sum_over_tensor(squares)
    scale_own = lax.rsqrt(squares / model_width + norm_epsilon)
    scale_far = across(scale_own)
    scales = (scale_own, scale_far)

    squeeze_half = squeeze_master.astype(bf16)
    squeeze_slab = both_cores(squeeze_half, across(squeeze_half))
    low_rank = low_rank_call(activations, scale_own, gain, squeeze_slab)
    low_rank = sum_over_tensor(low_rank)
    low_own = low_rank.astype(bf16)
    low_far = across(low_own)

    def with_far(act, cot):
        return (act, cot, across(act), across(cot))

    own_slab = with_far(act_hbm, cot_hbm)
    act_far = own_slab[2]
    gate_weight = resident(gate_frozen_weight)
    up_weight = resident(up_frozen_weight)
    weights = (gate_weight, up_weight, down_weight)
    sums = forward_call(size, [0], [own_slab], scales, gain, weights, None, None)
    for step in range(1, half):
        a_r, c_r, a_l, c_l = got[step - 1]
        slabs = [with_far(a_r, c_r), with_far(a_l, c_l)]
        sums = forward_call(size, [-step, step], slabs, scales, gain, weights, sums, None)
    a_r, c_l = got[half - 1]
    gate_grad, up_grad, low_part, low_other = forward_call(
        size,
        [half],
        [with_far(a_r, c_l)],
        scales,
        gain,
        weights,
        sums,
        (low_own, low_far, expand_state[0]),
    )
    grads = (gate_grad, up_grad)

    low_sum = sum_over_tensor(low_part + across(low_other))
    low_grad_own = low_sum[:rows].astype(bf16)
    low_grad_far = across(low_grad_own)

    pair = weights[:2]
    own, other = backward_call(size, [half], grads, pair, width)
    send_r, send_l = first_sends(own, across(other))
    got_r, got_l = lax.optimization_barrier((to_right(send_r), to_left(send_l)))
    for distance in range(half - 1, 0, -1):
        ro, rx, lo, lx = backward_call(size, [distance, -distance], grads, pair, width)
        send_r, send_l = next_sends((ro, across(rx)), (lo, across(lx)), (got_r, got_l))
        step = half - distance + 1
        got_r, got_l = lax.optimization_barrier((to_right(send_r), to_left(send_l)))
    own, other = backward_call(size, [0], grads, pair, width)

    expand_outs = expand_call(
        grads, low_own, low_far, *expand_state
    )
    squeeze_outs = squeeze_call(
        low_grad_own,
        low_grad_far,
        activations,
        act_far,
        scales,
        gain,
        *squeeze_state,
    )
    adapter_half = squeeze_outs[3]
    squeeze_adapter = both_cores(adapter_half, across(adapter_half))
    input_grad = input_grad_call(
        own,
        across(other),
        (got_r, got_l),
        activations,
        scale_own,
        gain,
        low_grad_own,
        low_rank,
        low_sum,
        squeeze_slab,
    )
    return (input_grad, *squeeze_outs[:3], squeeze_adapter, *expand_outs)


def solution(mesh):
    placed = (
        P(("groups", "dp"), "tensor"),
        P(),
        P(("tensor", "dp"), None),
        P(("tensor", "dp"), None),
        P(("tensor", "dp"), None),
        P(("groups", "dp"), "tensor"),
        P("groups", ("tensor", "dp")),
        P("groups", ("tensor", "dp")),
        P("groups", ("tensor", "dp")),
        P(("groups", "tensor", "dp"), None),
        P(("groups", "tensor", "dp"), None),
        P(("groups", "tensor", "dp"), None),
    )
    size = mesh.shape["tensor"]

    def body(*args):
        return on_device(size, *args)

    return jax.shard_map(
        body,
        mesh=mesh,
        in_specs=placed,
        out_specs=(
            P(("groups", "dp"), "tensor"),
            P("groups", ("tensor", "dp")),
            P("groups", ("tensor", "dp")),
            P("groups", ("tensor", "dp")),
            P("groups", "tensor"),
            P(("groups", "tensor", "dp"), None),
            P(("groups", "tensor", "dp"), None),
            P(("groups", "tensor", "dp"), None),
            P(("groups", "tensor", "dp"), None),
        ),
        check_vma=False,
    )
```
